32 devices in a mesh: gx: 4 (over y, x), gy: 4 (over z), gz: 2 (over core).
Axes of the slice: x: 2, y: 2, z: 4, core: 2. Of those that a mesh axis runs over, the one named last changes fastest.
Arguments:
- metric: float32 [6, 64, 128, 256], P(None, 'gx', 'gy', 'gz'), may hold values from -0.9 to 3, as said below
- mass: float32 [64, 128, 256], P('gx', 'gy', 'gz'), may hold values from 0.5 to 2
- shift: float32 [1], replicated, may hold values from 20 to 80
- loads: float32 [4, 64, 128, 256], P(None, 'gx', 'gy', 'gz'), may hold values from -16 to 16
- inputs: float32 [4, 64, 128, 256], P(None, 'gx', 'gy', 'gz'), may hold values from -0.2762136 to 0.2762136
Outputs:
- residual_factor: float32 [4, 64, 128, 256], P(None, 'gx', 'gy', 'gz')
- feedback: float32 [4, 64, 128, 256], P(None, 'gx', 'gy', 'gz')
The draws below stay inside these ranges and needn't reach their ends.
Inputs may be any that keep to these rules, and one draw needn't show every extreme that they name: `metric`: each node's six factors form a symmetric positive definite matrix: diagonal entries between 0.3 and 3, off-diagonal entries at most 0.3 times the geometric mean of their two diagonal entries in magnitude.
All inputs are finite; a program needn't handle non-finite values.
Results may differ from the reference program's by a relative error of at most 0.00029.
Values sent between devices are 32-bit elements; how exact they have to be, the bound alone decides.
A program may use at most 128 MiB of HBM per device.

```python
import math
import jax
import jax.numpy as jnp
import numpy as np
from jax import lax

COLUMNS = 4
INPUTS = 4
STEPS = 5
NX = 64
NY = 128
NZ = 256


def ramp_profile():
    first = jnp.arange(NX, dtype=jnp.float32) / NX
    second = jnp.arange(NY, dtype=jnp.float32) / NY
    third = jnp.arange(NZ, dtype=jnp.float32) / NZ
    return 0.5 * (1.0 + first)[:, None, None] * (1.0 + second)[None, :, None] * (1.0 + third)[None, None, :]


def rough_field(key, salt, count, factor):
    key = jax.random.fold_in(key, salt)
    shape = (count, NX, NY, NZ)
    base = jnp.clip(jax.random.normal(key, shape, jnp.float32), -4.0, 4.0)
    return base * ramp_profile()[None] * factor


def draw_loads(key, part):
    return rough_field(key, 11, COLUMNS, 1.0)


def draw_inputs(key, part):
    return rough_field(key, 23, INPUTS, 25.0 / math.sqrt(NX * NY * NZ))


def draw_metric(key, part):
    first, second = jax.random.split(jax.random.fold_in(key, 37), 2)
    shape = (3, NX, NY, NZ)
    levels = jax.random.uniform(first, shape, jnp.float32, 0.0, 1.0)
    diagonal = 0.3 * jnp.exp(levels * math.log(10.0))
    ratio = jax.random.uniform(second, shape, jnp.float32, -0.3, 0.3)
    cross_one = ratio[0] * jnp.sqrt(diagonal[0] * diagonal[1])
    cross_two = ratio[1] * jnp.sqrt(diagonal[0] * diagonal[2])
    cross_three = ratio[2] * jnp.sqrt(diagonal[1] * diagonal[2])
    return jnp.stack([diagonal[0], diagonal[1], diagonal[2], cross_one, cross_two, cross_three], 0)


def steps_of(own_key, dims, shards, low, top_value):
    factor_of = 1.0
    for axis_at, parts in shards:
        draws = jax.random.uniform(jax.random.fold_in(jax.random.fold_in(own_key, 6), axis_at), (parts,), jnp.float32, low / len(shards), top_value / len(shards))
        factor_of = factor_of * jnp.repeat(jnp.exp(draws), dims[axis_at] // parts).reshape((-1,) + (1,) * (len(dims) - 1 - axis_at))
    return factor_of


def setup_inputs(seed: int = 0) -> dict:
    key_of = jax.random.split(jax.random.key(seed), 6)
    return {
        "metric": draw_metric(jax.random.fold_in(key_of[5], 71), 0),
        "mass": jnp.clip(jnp.exp(math.log(2.0) - 1.3862944 * jax.random.uniform(key_of[1], (NX, NY, NZ), jnp.float32) ** steps_of(key_of[1], (NX, NY, NZ), ((0, 4), (1, 4), (2, 2)), -0.2, 0.2)), 0.5, 2.0),
        "shift": jnp.clip(jax.random.uniform(key_of[2], (1,), jnp.float32, 20.0, 80.0), 20.0, 80.0),
        "loads": draw_loads(jax.random.fold_in(key_of[5], 71), 0),
        "inputs": draw_inputs(jax.random.fold_in(key_of[5], 71), 0),
    }


gll_points = (-1.0, -0.8717401485096066, -0.5917001814331423, -0.2092992179024789, 0.2092992179024789, 0.5917001814331423, 0.8717401485096066, 1.0)
gll_ends = (-14.0, 0.0, 0.0, 0.0, 0.0, 0.0, 0.0, 14.0)

def gll_table():
    points = np.array(gll_points)
    values = (429.0 * points ** 7 - 693.0 * points ** 5 + 315.0 * points ** 3 - 35.0 * points) / 16.0
    table = np.zeros((8, 8))
    for row in range(8):
        for column in range(8):
            if row != column:
                table[row, column] = values[row] / (values[column] * (points[row] - points[column]))
    table[0, 0] = -14.0
    table[7, 7] = 14.0
    return table

def derive_first(field, matrix):
    width, height, depth = field.shape
    shaped = field.reshape(width // 8, 8, height, depth)
    return jnp.einsum('ma,eayz->emyz', matrix, shaped, precision=lax.Precision.HIGHEST).reshape(field.shape)

def derive_second(field, matrix):
    width, height, depth = field.shape
    shaped = field.reshape(width, height // 8, 8, depth)
    return jnp.einsum('mb,xebz->xemz', matrix, shaped, precision=lax.Precision.HIGHEST).reshape(field.shape)

def derive_third(field, matrix):
    width, height, depth = field.shape
    shaped = field.reshape(width, height, depth // 8, 8)
    return jnp.einsum('mk,xyek->xyem', matrix, shaped, precision=lax.Precision.HIGHEST).reshape(field.shape)

def pair_fold(padded, dim):
    length = padded.shape[dim] - 2
    phase = jnp.arange(length) % 8
    shape = [1] * padded.ndim
    shape[dim] = length
    upper = (phase == 7).reshape(shape)
    lower = (phase == 0).reshape(shape)
    middle = lax.slice_in_dim(padded, 1, length + 1, axis=dim)
    after = lax.slice_in_dim(padded, 2, length + 2, axis=dim)
    before = lax.slice_in_dim(padded, 0, length, axis=dim)
    return middle + jnp.where(upper, after, 0.0) + jnp.where(lower, before, 0.0)

def assemble_one(field):
    for dim in (0, 1, 2):
        widths = [(0, 0), (0, 0), (0, 0)]
        widths[dim] = (1, 1)
        field = pair_fold(jnp.pad(field, widths), dim)
    return field

def assemble(stack):
    return lax.map(assemble_one, stack)

def column_apply(field, metric, scaled_mass, table):
    slope_first = derive_first(field, table)
    slope_second = derive_second(field, table)
    slope_third = derive_third(field, table)
    flux_first = metric[0] * slope_first + metric[3] * slope_second + metric[4] * slope_third
    flux_second = metric[3] * slope_first + metric[1] * slope_second + metric[5] * slope_third
    flux_third = metric[4] * slope_first + metric[5] * slope_second + metric[2] * slope_third
    result = derive_first(flux_first, table.T) + derive_second(flux_second, table.T)
    return result + derive_third(flux_third, table.T) + scaled_mass * field

def reference(metric, mass, shift, loads, inputs):
    table_np = gll_table()
    table = jnp.asarray(table_np, jnp.float32)
    squares = table * table
    width, height, depth = mass.shape
    ends_np = np.array(gll_ends)
    ends_first = jnp.asarray(np.tile(ends_np, width // 8), jnp.float32)[:, None, None]
    ends_second = jnp.asarray(np.tile(ends_np, height // 8), jnp.float32)[None, :, None]
    ends_third = jnp.asarray(np.tile(ends_np, depth // 8), jnp.float32)[None, None, :]
    scale = shift[0]
    scaled_mass = scale * mass
    jdiag = derive_first(metric[0], squares.T) + derive_second(metric[1], squares.T) + derive_third(metric[2], squares.T)
    cross = ends_first * ends_second * metric[3] + ends_first * ends_third * metric[4] + ends_second * ends_third * metric[5]
    jdiag = jdiag + 2.0 * cross + scaled_mass
    stacked = jnp.concatenate([jnp.ones((1, width, height, depth), jnp.float32), jdiag[None], mass[None], loads, inputs], 0)
    assembled = assemble(stacked)
    columns = loads.shape[0]
    weight = 1.0 / assembled[0]
    precond = 1.0 / assembled[1]
    mtotal = assembled[2]
    rhs = assembled[3:3 + columns]
    drive = assembled[3 + columns:]

    def operate(field):
        return assemble(lax.map(lambda single: column_apply(single, metric, scaled_mass, table), field))

    def products(first, second):
        return jnp.sum(first * second * weight, axis=(1, 2, 3))
    solution = jnp.zeros_like(rhs)
    residual = rhs
    smooth = precond * residual
    direction = smooth
    energy = products(residual, smooth)
    for step in range(STEPS):
        image = operate(direction)
        alpha = energy / products(direction, image)
        solution = solution + alpha[:, None, None, None] * direction
        residual = residual - alpha[:, None, None, None] * image
        smooth = precond * residual
        fresh = products(residual, smooth)
        direction = smooth + (fresh / energy)[:, None, None, None] * direction
        energy = fresh
    coupling = jnp.einsum('cxyz,jxyz->cj', solution * weight, drive, precision=lax.Precision.HIGHEST)
    identity = jnp.eye(columns, dtype=jnp.float32)
    ymat = identity + jnp.dot(coupling, coupling.T, precision=lax.Precision.HIGHEST)
    factor = jnp.linalg.cholesky(ymat)
    inverse = jax.scipy.linalg.cho_solve((factor, True), identity)
    gain_coef = jax.scipy.linalg.cho_solve((factor, True), coupling)
    heat = mtotal * solution
    twice = 2.0 * scale
    residual_factor = rhs - twice * jnp.einsum('cxyz,cj->jxyz', heat, inverse, precision=lax.Precision.HIGHEST)
    feedback = twice * jnp.einsum('cxyz,cj->jxyz', heat, gain_coef, precision=lax.Precision.HIGHEST)
    return (residual_factor, feedback)
```

```python
import functools

import jax
import jax.numpy as jnp
import numpy as np
from jax import lax
from jax.experimental import pallas as pl
from jax.experimental.pallas import tpu as pltpu
from jax.sharding import PartitionSpec as P

STEPS = 5
MESH = pl.DeviceIdType.MESH
F32 = jnp.float32
BF16 = jnp.bfloat16

gll_points = (
    -1.0,
    -0.8717401485096066,
    -0.5917001814331423,
    -0.2092992179024789,
    0.2092992179024789,
    0.5917001814331423,
    0.8717401485096066,
    1.0,
)


def gll_table():
    points = np.array(gll_points)
    values = (429.0 * points**7 - 693.0 * points**5 + 315.0 * points**3 - 35.0 * points) / 16.0
    table = np.zeros((8, 8))
    for row in range(8):
        for column in range(8):
            if row != column:
                table[row, column] = values[row] / (values[column] * (points[row] - points[column]))
    table[0, 0] = -14.0
    table[7, 7] = 14.0
    return table


TABLE = gll_table()


def halves(matrix):
    full = np.asarray(matrix, np.float32)
    high = full.astype(jnp.bfloat16)
    low = (full - high.astype(np.float32)).astype(jnp.bfloat16)
    return high, low


def left_matrices(height):
    eye = np.eye(height)
    squares = TABLE * TABLE
    return np.stack([np.stack(halves(np.kron(eye, m))) for m in (TABLE, TABLE.T, squares.T)])


def right_matrices(depth):
    eye = np.eye(depth // 8)
    squares = TABLE * TABLE
    out = []
    for m in (TABLE.T, TABLE, squares):
        high, low = halves(np.kron(eye, m))
        out.append(np.block([[high, low], [high, np.zeros_like(low)]]))
    return np.stack(out)


def mix_lines(matrix, lines):
    even = [lines[j] + lines[7 - j] for j in range(4)]
    odd = [lines[j] - lines[7 - j] for j in range(4)]
    out = [None] * 8
    for i in range(4):
        p = q = None
        for j in range(4):
            a = float(np.float32(0.5 * (matrix[i, j] + matrix[i, 7 - j])))
            b = float(np.float32(0.5 * (matrix[i, j] - matrix[i, 7 - j])))
            p = a * even[j] if p is None else p + a * even[j]
            q = b * odd[j] if q is None else q + b * odd[j]
        out[i] = q + p
        out[7 - i] = q - p
    return out


def split(v):
    high = v.astype(BF16)
    low = (v - high.astype(F32)).astype(BF16)
    return high, low


def dot(a, b):
    return jnp.dot(a, b, preferred_element_type=F32)


def left_apply(ly, kind, v):
    high, low = split(v)
    return (dot(ly[kind, 0], low) + dot(ly[kind, 1], high)) + dot(ly[kind, 0], high)


def right_apply(lz, kind, v):
    high, low = split(v)
    depth = v.shape[1]
    both = dot(jnp.concatenate([high, low], axis=1), lz[kind])
    return both[:, :depth] + both[:, depth:]


def fold8(v):
    total = v[0:8]
    for k in range(1, v.shape[0] // 8):
        total = total + v[8 * k : 8 * k + 8]
    return total


def kernel(
    dims, counts,
    metric, mass, shift, loads, inputs, ly, lz,
    rf, fb,
    lv, z, p, s, xs, r, wgt, pre, mtot, s2, s3, f2, f3, rr, acc, rows, state,
    zsend0, zrecv0, xsend0, xrecv0, ysend0, yrecv0, esend0, erecv0,
    zsend, zrecv, xsend, xrecv, ysend, yrecv, esend, erecv,
    asend, arecv,
    send0, recv0, send1, recv1, sendr, recvr,
):
    C, X, Y, Z = dims
    nx, ny, nz = counts
    N = nx * ny * nz
    E = X // 8
    R = 8 * Y
    XY = X * Y
    gx, gy, gz = lax.axis_index("gx"), lax.axis_index("gy"), lax.axis_index("gz")
    me = (gx * ny + gy) * nz + gz
    sh = shift[0]
    lane = lax.broadcasted_iota(jnp.int32, (8, Z), 1)

    def coords(number):
        rest = lax.div(number, nz)
        return (lax.div(rest, ny), lax.rem(rest, ny), lax.rem(number, nz))

    for ref in (zrecv0, xrecv0, yrecv0, erecv0, zrecv, xrecv, yrecv, erecv, esend0, esend):
        ref[...] = jnp.zeros(ref.shape, F32)

    barrier = pltpu.get_barrier_semaphore()

    def greet(i, carry):
        pl.semaphore_signal(
            barrier, inc=1, device_id=coords(lax.rem(me + i, N)), device_id_type=MESH
        )
        return carry

    lax.fori_loop(1, N, greet, 0)

    low_z = gz > 0
    high_z = gz < nz - 1
    low_of = {"x": gx > 0, "y": gy > 0}
    high_of = {"x": gx < nx - 1, "y": gy < ny - 1}
    inner0 = (lane % 8 == 0) & (lane > 0)
    inner7 = (lane % 8 == 7) & (lane < Z - 1)
    rim = (lane == 0) | (lane == Z - 1)

    def assemble(ncols, bufs, sems, par):
        zs, zr, xsn, xr, ysn, yr, es, er = bufs
        ssem, rsem = sems
        for c in range(ncols):
            for e in range(1, E):
                a = (c * X + 8 * e - 1) * Y
                t = lv[a : a + Y] + lv[a + Y : a + 2 * Y]
                lv[a : a + Y] = t
                lv[a + Y : a + 2 * Y] = t
        for k in range(1, Y // 8):
            first = pl.ds(8 * k - 1, ncols * X, stride=Y)
            second = pl.ds(8 * k, ncols * X, stride=Y)
            t = lv[first, :] + lv[second, :]
            lv[first, :] = t
            lv[second, :] = t

        def fold(c, carry):
            packed = jnp.zeros((8, Z), F32)
            for k in range(XY // 8):
                at = pl.ds(pl.multiple_of(c * XY + 8 * k, 8), 8)
                v = lv[at, :]
                v = v + jnp.where(
                    inner0, pltpu.roll(v, 1, 1), jnp.where(inner7, pltpu.roll(v, Z - 1, 1), 0.0)
                )
                lv[at, :] = v
                q = 2 * k
                moved = pltpu.roll(v, q, 1) if q else v
                packed = jnp.where((lane == q) | (lane == (q - 1) % Z), moved, packed)
            zs[pl.ds(pl.multiple_of(8 * c, 8), 8), :] = packed
            return carry

        lax.fori_loop(0, ncols, fold, 0)

        def zcopy(h):
            return pltpu.make_async_remote_copy(
                src_ref=zs,
                dst_ref=zr.at[par, 1 - h],
                send_sem=ssem.at[par, h],
                recv_sem=rsem.at[par, 1 - h],
                device_id=(gx, gy, gz + (2 * h - 1)),
                device_id_type=MESH,
            )

        zgoes = (low_z, high_z)
        for h in range(2):
            @pl.when(zgoes[h])
            def _():
                zcopy(h).start()
        for h in range(2):
            @pl.when(zgoes[1 - h])
            def _():
                zcopy(h).wait_recv()

        def unfold(c, carry):
            at = pl.ds(pl.multiple_of(8 * c, 8), 8)
            from_low = zr[par, 0, at, :]
            from_high = zr[par, 1, at, :]
            both = jnp.where(
                lane % 2 == 0, pltpu.roll(from_low, 1, 1), pltpu.roll(from_high, Z - 1, 1)
            )
            for k in range(XY // 8):
                at = pl.ds(pl.multiple_of(c * XY + 8 * k, 8), 8)
                q = (Z - 2 * k) % Z
                moved = pltpu.roll(both, q, 1) if q else both
                lv[at, :] = lv[at, :] + jnp.where(rim, moved, 0.0)
            return carry

        lax.fori_loop(0, ncols, unfold, 0)

        edge = (0, X - 1), (0, Y - 1)
        for h in range(2):
            for c in range(ncols):
                a = (c * X + edge[0][h]) * Y
                xsn[h, c * Y : (c + 1) * Y, :] = lv[a : a + Y]
            ysn[h] = lv[pl.ds(edge[1][h], ncols * X, stride=Y), :]
        for hx in range(2):
            for hy in range(2):
                for c in range(ncols):
                    a = (c * X + edge[0][hx]) * Y + edge[1][hy]
                    es[2 * hx + hy, c : c + 1, :] = lv[a : a + 1, :]

        plans = []
        for h in range(2):
            d = 2 * h - 1
            plans.append((
                (high_of if h else low_of)["x"], (low_of if h else high_of)["x"],
                xsn.at[h], xr.at[par, 1 - h], 2 + h, 2 + (1 - h), (gx + d, gy, gz),
            ))
            plans.append((
                (high_of if h else low_of)["y"], (low_of if h else high_of)["y"],
                ysn.at[h], yr.at[par, 1 - h], 4 + h, 4 + (1 - h), (gx, gy + d, gz),
            ))
        for hx in range(2):
            for hy in range(2):
                goes = (high_of if hx else low_of)["x"] & (high_of if hy else low_of)["y"]
                comes = (low_of if hx else high_of)["x"] & (low_of if hy else high_of)["y"]
                slot = 2 * (1 - hx) + (1 - hy)
                plans.append((
                    goes, comes, es.at[2 * hx + hy], er.at[par, slot],
                    6 + 2 * hx + hy, 6 + slot, (gx + 2 * hx - 1, gy + 2 * hy - 1, gz),
                ))

        def copy_of(plan):
            return pltpu.make_async_remote_copy(
                src_ref=plan[2],
                dst_ref=plan[3],
                send_sem=ssem.at[par, plan[4]],
                recv_sem=rsem.at[par, plan[5]],
                device_id=plan[6],
                device_id_type=MESH,
            )

        for plan in plans:
            @pl.when(plan[0])
            def _():
                copy_of(plan).start()
        for plan in plans:
            @pl.when(plan[1])
            def _():
                copy_of(plan).wait_recv()
        for h in range(2):
            for c in range(ncols):
                a = (c * X + edge[0][h]) * Y
                lv[a : a + Y] = lv[a : a + Y] + xr[par, h, c * Y : (c + 1) * Y, :]
            at = pl.ds(edge[1][h], ncols * X, stride=Y)
            lv[at, :] = lv[at, :] + yr[par, h]
        for hx in range(2):
            for hy in range(2):
                for c in range(ncols):
                    a = (c * X + edge[0][hx]) * Y + edge[1][hy]
                    lv[a : a + 1, :] = lv[a : a + 1, :] + er[par, 2 * hx + hy, c : c + 1, :]
        for h in range(2):
            @pl.when(zgoes[h])
            def _():
                zcopy(h).wait_send()
        for plan in plans:
            @pl.when(plan[0])
            def _():
                copy_of(plan).wait_send()

    squares = TABLE * TABLE
    row_of = lax.broadcasted_iota(jnp.int32, (Y, Z), 0)
    lane_of = lax.broadcasted_iota(jnp.int32, (Y, Z), 1)
    at_zero, at_seven = row_of % 8 == 0, row_of % 8 == 7
    ends_y = jnp.where(at_zero, -14.0, jnp.where(at_seven, 14.0, 0.0))
    ends_z = jnp.where(lane_of % 8 == 0, -14.0, jnp.where(lane_of % 8 == 7, 14.0, 0.0))
    wide = jnp.where(at_zero | at_seven, 0.5, 1.0)
    wide = jnp.where((row_of == 0) & (gy == 0), 1.0, wide)
    wide = jnp.where((row_of == Y - 1) & (gy == ny - 1), 1.0, wide)
    deep = jnp.where((lane_of % 8 == 0) | (lane_of % 8 == 7), 0.5, 1.0)
    deep = jnp.where((lane_of == 0) & (gz == 0), 1.0, deep)
    deep = jnp.where((lane_of == Z - 1) & (gz == nz - 1), 1.0, deep)
    plane = wide * deep
    for x in range(X):
        if x == 0:
            factor = jnp.where(gx > 0, 0.5, 1.0)
        elif x == X - 1:
            factor = jnp.where(gx < nx - 1, 0.5, 1.0)
        else:
            factor = 0.5 if x % 8 in (0, 7) else 1.0
        wgt[x * Y : (x + 1) * Y] = plane * factor

    lv[0 : C * XY] = loads[...]
    lv[(C + 1) * XY : (C + 2) * XY] = mass[...]
    for e in range(E):
        base = e * R
        rr[...] = left_apply(ly, 2, metric[1, base : base + R, :]) + right_apply(
            lz, 2, metric[2, base : base + R, :]
        )
        for i in range(8):
            a = base + i * Y
            total = rr[i * Y : (i + 1) * Y] + sh * mass[a : a + Y]
            for m in range(8):
                w = float(np.float32(squares[m, i]))
                if w != 0.0:
                    total = total + w * metric[0, base + m * Y : base + (m + 1) * Y, :]
            cross = ends_y * ends_z * metric[5, a : a + Y, :]
            if i in (0, 7):
                end = -14.0 if i == 0 else 14.0
                cross = cross + end * (
                    ends_y * metric[3, a : a + Y, :] + ends_z * metric[4, a : a + Y, :]
                )
            lv[C * XY + a : C * XY + a + Y] = total + 2.0 * cross
    zero = jnp.zeros((C * XY, Z), F32)
    p[...] = zero
    s[...] = zero
    xs[...] = zero
    rows[...] = jnp.zeros(rows.shape, F32)
    state[...] = jnp.zeros(state.shape, F32)

    pl.semaphore_wait(barrier, N - 1)
    assemble(
        C + 2,
        (zsend0, zrecv0, xsend0, xrecv0, ysend0, yrecv0, esend0, erecv0),
        (send0, recv0), 0,
    )
    rf[...] = lv[0 : C * XY]
    r[...] = lv[0 : C * XY]
    pre[...] = 1.0 / lv[C * XY : (C + 1) * XY]
    mtot[...] = lv[(C + 1) * XY : (C + 2) * XY]
    for c in range(C):
        z[c * XY : (c + 1) * XY] = pre[...] * lv[c * XY : (c + 1) * XY]

    def slab(i, carry):
        c = lax.div(i, E)
        e = i - c * E
        base = pl.multiple_of(i * R, R)
        ebase = pl.multiple_of(e * R, R)
        v = z[pl.ds(base, R), :]
        s2[...] = left_apply(ly, 0, v)
        s3[...] = right_apply(lz, 0, v)
        for t in range(Y // 8):
            va = [z[pl.ds(pl.multiple_of(base + a * Y + 8 * t, 8), 8), :] for a in range(8)]
            s1 = mix_lines(TABLE, va)
            f1 = []
            for m in range(8):
                o = m * Y + 8 * t
                at = pl.ds(pl.multiple_of(ebase + o, 8), 8)
                a, b, g = s1[m], s2[o : o + 8, :], s3[o : o + 8, :]
                m12, m13, m23 = metric[3, at, :], metric[4, at, :], metric[5, at, :]
                f1.append(metric[0, at, :] * a + m12 * b + m13 * g)
                f2[o : o + 8, :] = m12 * a + metric[1, at, :] * b + m23 * g
                f3[o : o + 8, :] = m13 * a + m23 * b + metric[2, at, :] * g
            r1 = mix_lines(TABLE.T, f1)
            for a in range(8):
                o = a * Y + 8 * t
                at = pl.ds(pl.multiple_of(ebase + o, 8), 8)
                rr[o : o + 8, :] = r1[a] + (sh * mass[at, :]) * va[a]
        out = rr[...] + left_apply(ly, 1, f2[...]) + right_apply(lz, 1, f3[...])
        lv[pl.ds(base, R), :] = out
        v = z[pl.ds(base, R), :]
        keep = jnp.where(e == 0, 0.0, 1.0)
        for j in range(C):
            term = fold8(v * inputs[pl.ds(pl.multiple_of(j * XY + ebase, R), R), :])
            acc[C * c + j] = keep * acc[C * c + j] + term
        term = fold8(wgt[pl.ds(ebase, R), :] * (r[pl.ds(base, R), :] * v))
        acc[C * C + c] = keep * acc[C * C + c] + term
        term = fold8(out * v)
        acc[C * C + C + c] = keep * acc[C * C + C + c] + term
        return carry

    def reduce_copy(i, par):
        peer = lax.rem(me + i, N)
        return pltpu.make_async_remote_copy(
            src_ref=asend,
            dst_ref=arecv.at[par, me],
            send_sem=sendr.at[i],
            recv_sem=recvr.at[par, me],
            device_id=coords(peer),
            device_id_type=MESH,
        )

    def arrive_copy(i, par):
        peer = lax.rem(me + i, N)
        return pltpu.make_async_remote_copy(
            src_ref=asend,
            dst_ref=arecv.at[par, peer],
            send_sem=sendr.at[i],
            recv_sem=recvr.at[par, peer],
            device_id=coords(peer),
            device_id_type=MESH,
        )

    def step(number, carry):
        par = lax.rem(number, 2)
        acc[...] = jnp.zeros(acc.shape, F32)
        lax.fori_loop(0, C * E, slab, 0)
        for c in range(C):
            for j in range(C):
                q = C * c + j
                rows[q : q + 1, :] = jnp.sum(acc[q], axis=0, keepdims=True)
            energy = jnp.sum(acc[C * C + c], axis=0, keepdims=True)
            curve = jnp.sum(acc[C * C + C + c], axis=0, keepdims=True)
            for j in range(C):
                q = C * c + j
                rows[C * C + q : C * C + q + 1, :] = energy
                rows[2 * C * C + q : 2 * C * C + q + 1, :] = curve
        part = jnp.sum(rows[...].T, axis=0, keepdims=True)
        asend[...] = part
        arecv[par, me] = part

        def push(i, carry):
            reduce_copy(i, par).start()
            return carry

        lax.fori_loop(1, N, push, 0)
        assemble(
            C,
            (zsend, zrecv, xsend, xrecv, ysend, yrecv, esend, erecv),
            (send1, recv1), par,
        )

        def gather(i, carry):
            arrive_copy(i, par).wait_recv()
            return carry

        lax.fori_loop(1, N, gather, 0)
        total = jnp.sum(arecv[par], axis=0)
        gamma = pltpu.roll(total, 128 - C * C, 1)
        delta = pltpu.roll(total, 128 - 2 * C * C, 1)
        used = lax.broadcasted_iota(jnp.int32, (1, 128), 1) < C * C
        gamma = jnp.where(used, gamma, 1.0)
        delta = jnp.where(used, delta, 1.0)
        fresh = number == 0
        old_gamma = jnp.where(fresh, 1.0, state[0:1, :])
        old_alpha = jnp.where(fresh, 1.0, state[1:2, :])
        beta = jnp.where(fresh, 0.0, gamma / old_gamma)
        alpha = gamma / (delta - beta * gamma / old_alpha)
        along = total + beta * state[2:3, :]
        state[0:1, :] = gamma
        state[1:2, :] = alpha
        state[2:3, :] = along
        state[3:4, :] = state[3:4, :] + alpha * along
        for c in range(C):
            b = jnp.broadcast_to(beta[:, C * c : C * c + 1], (Y, Z))
            a = jnp.broadcast_to(alpha[:, C * c : C * c + 1], (Y, Z))
            def update(x, carry):
                at = pl.ds(pl.multiple_of(c * XY + x * Y, Y), Y)
                pn = z[at, :] + b * p[at, :]
                sn = lv[at, :] + b * s[at, :]
                p[at, :] = pn
                s[at, :] = sn
                xs[at, :] = xs[at, :] + a * pn
                rn = r[at, :] - a * sn
                r[at, :] = rn
                z[at, :] = pre[pl.ds(pl.multiple_of(x * Y, Y), Y), :] * rn
                return carry
            lax.fori_loop(0, X, update, 0, unroll=4)

        def drain(i, carry):
            reduce_copy(i, par).wait_send()
            return carry

        lax.fori_loop(1, N, drain, 0)
        return carry

    lax.fori_loop(0, STEPS, step, 0)

    flat = state[3:4, :]
    k = [[flat[:, C * c + j : C * c + j + 1] for j in range(C)] for c in range(C)]
    y = [[None] * C for _ in range(C)]
    for a in range(C):
        for b in range(C):
            if b < a:
                y[a][b] = y[b][a]
                continue
            t = k[a][0] * k[b][0]
            for j in range(1, C):
                t = t + k[a][j] * k[b][j]
            y[a][b] = t + 1.0 if a == b else t
    one = jnp.ones((1, 1), F32)
    nil = jnp.zeros((1, 1), F32)
    right = [[one if a == b else nil for b in range(C)] + k[a] for a in range(C)]
    for a in range(C):
        inv = 1.0 / y[a][a]
        y[a] = [t * inv for t in y[a]]
        right[a] = [t * inv for t in right[a]]
        for b in range(C):
            if b != a:
                w = y[b][a]
                y[b] = [u - w * t for u, t in zip(y[b], y[a])]
                right[b] = [u - w * t for u, t in zip(right[b], right[a])]
    twice = 2.0 * sh
    coef = [[jnp.broadcast_to(twice * right[c][j], (8, Z)) for j in range(2 * C)] for c in range(C)]

    def finish(i, carry):
        at = pl.ds(pl.multiple_of(8 * i, 8), 8)
        m = mtot[at, :]
        heat = [m * xs[pl.ds(pl.multiple_of(c * XY + 8 * i, 8), 8), :] for c in range(C)]
        for j in range(C):
            at = pl.ds(pl.multiple_of(j * XY + 8 * i, 8), 8)
            t = heat[0] * coef[0][j]
            u = heat[0] * coef[0][C + j]
            for c in range(1, C):
                t = t + heat[c] * coef[c][j]
                u = u + heat[c] * coef[c][C + j]
            rf[at, :] = rf[at, :] - t
            fb[at, :] = u
        return carry

    lax.fori_loop(0, XY // 8, finish, 0, unroll=2)


def local(counts, metric, mass, shift, loads, inputs):
    C, X, Y, Z = loads.shape
    N = counts[0] * counts[1] * counts[2]
    XY = X * Y
    ly = jnp.asarray(left_matrices(Y))
    lz = jnp.asarray(right_matrices(Z))
    vm = lambda *shape: pltpu.VMEM(shape, F32)

    def comm(cols, pars):
        return [
            vm(8 * cols, Z), vm(pars, 2, 8 * cols, Z),
            vm(2, cols * Y, Z), vm(pars, 2, cols * Y, Z),
            vm(2, cols * X, Z), vm(pars, 2, cols * X, Z),
            vm(4, 8, Z), vm(pars, 4, 8, Z),
        ]

    dma = pltpu.SemaphoreType.DMA
    spec = pl.BlockSpec(memory_space=pltpu.VMEM)
    rf, fb = pl.pallas_call(
        functools.partial(kernel, (C, X, Y, Z), counts),
        out_shape=[jax.ShapeDtypeStruct((C * XY, Z), F32)] * 2,
        in_specs=[spec, spec, pl.BlockSpec(memory_space=pltpu.SMEM), spec, spec, spec, spec],
        out_specs=[spec, spec],
        scratch_shapes=[
            vm((C + 2) * XY, Z), vm(C * XY, Z), vm(C * XY, Z), vm(C * XY, Z), vm(C * XY, Z),
            vm(C * XY, Z), vm(XY, Z), vm(XY, Z), vm(XY, Z),
            vm(8 * Y, Z), vm(8 * Y, Z), vm(8 * Y, Z), vm(8 * Y, Z), vm(8 * Y, Z),
            vm(C * C + 2 * C, 8, Z), vm(128, Z), vm(8, 128),
        ]
        + comm(C + 2, 1)
        + comm(C, 2)
        + [vm(1, 128), vm(2, N, 1, 128)]
        + [dma((1, 10)), dma((1, 10)), dma((2, 10)), dma((2, 10)), dma((N,)), dma((2, N))],
        compiler_params=pltpu.CompilerParams(
            collective_id=0, has_side_effects=True, vmem_limit_bytes=56 << 20
        ),
    )(
        metric.reshape(6, XY, Z), mass.reshape(XY, Z), shift,
        loads.reshape(C * XY, Z), inputs.reshape(C * XY, Z), ly, lz,
    )
    return (rf.reshape(loads.shape), fb.reshape(loads.shape))


def solution(mesh):
    counts = tuple(mesh.shape[a] for a in ("gx", "gy", "gz"))
    return jax.shard_map(
        functools.partial(local, counts),
        mesh=mesh,
        in_specs=(
            P(None, "gx", "gy", "gz"),
            P("gx", "gy", "gz"),
            P(),
            P(None, "gx", "gy", "gz"),
            P(None, "gx", "gy", "gz"),
        ),
        out_specs=(P(None, "gx", "gy", "gz"), P(None, "gx", "gy", "gz")),
        check_vma=False,
    )
```

```python
import functools

import jax
import jax.numpy as jnp
import numpy as np
from jax import lax
from jax.experimental import pallas as pl
from jax.experimental.pallas import tpu as pltpu
from jax.sharding import PartitionSpec as P

STEPS = 5
MESH = pl.DeviceIdType.MESH
F32 = jnp.float32
BF16 = jnp.bfloat16

gll_points = (
    -1.0,
    -0.8717401485096066,
    -0.5917001814331423,
    -0.2092992179024789,
    0.2092992179024789,
    0.5917001814331423,
    0.8717401485096066,
    1.0,
)


def gll_table():
    points = np.array(gll_points)
    values = (429.0 * points**7 - 693.0 * points**5 + 315.0 * points**3 - 35.0 * points) / 16.0
    table = np.zeros((8, 8))
    for row in range(8):
        for column in range(8):
            if row != column:
                table[row, column] = values[row] / (values[column] * (points[row] - points[column]))
    table[0, 0] = -14.0
    table[7, 7] = 14.0
    return table


TABLE = gll_table()


def halves(matrix):
    full = np.asarray(matrix, np.float32)
    high = full.astype(jnp.bfloat16)
    low = (full - high.astype(np.float32)).astype(jnp.bfloat16)
    return high, low


def left_matrices(height):
    eye = np.eye(height)
    squares = TABLE * TABLE
    return np.stack([np.stack(halves(np.kron(eye, m))) for m in (TABLE, TABLE.T, squares.T)])


def right_matrices(depth):
    eye = np.eye(depth // 8)
    squares = TABLE * TABLE
    out = []
    for m in (TABLE.T, TABLE, squares):
        high, low = halves(np.kron(eye, m))
        out.append(np.block([[high, low], [high, np.zeros_like(low)]]))
    return np.stack(out)


def mix_lines(matrix, lines):
    even = [lines[j] + lines[7 - j] for j in range(4)]
    odd = [lines[j] - lines[7 - j] for j in range(4)]
    out = [None] * 8
    for i in range(4):
        p = q = None
        for j in range(4):
            a = float(np.float32(0.5 * (matrix[i, j] + matrix[i, 7 - j])))
            b = float(np.float32(0.5 * (matrix[i, j] - matrix[i, 7 - j])))
            p = a * even[j] if p is None else p + a * even[j]
            q = b * odd[j] if q is None else q + b * odd[j]
        out[i] = q + p
        out[7 - i] = q - p
    return out


def split(v):
    high = v.astype(BF16)
    low = (v - high.astype(F32)).astype(BF16)
    return high, low


def dot(a, b):
    return jnp.dot(a, b, preferred_element_type=F32)


def left_apply(ly, kind, v):
    high, low = split(v)
    return (dot(ly[kind, 0], low) + dot(ly[kind, 1], high)) + dot(ly[kind, 0], high)


def right_apply(lz, kind, v):
    high, low = split(v)
    depth = v.shape[1]
    both = dot(jnp.concatenate([high, low], axis=1), lz[kind])
    return both[:, :depth] + both[:, depth:]


def fold8(v):
    total = v[0:8]
    for k in range(1, v.shape[0] // 8):
        total = total + v[8 * k : 8 * k + 8]
    return total


def kernel(
    dims, counts,
    metric, mass, shift, loads, inputs, ly, lz,
    rf, fb,
    lv, z, p, s, xs, r, wgt, pre, mtot, s2, s3, f2, f3, rr, acc, rows, state,
    zsend0, zrecv0, xsend0, xrecv0, ysend0, yrecv0, esend0, erecv0,
    zsend, zrecv, xsend, xrecv, ysend, yrecv, esend, erecv,
    asend, arecv,
    send0, recv0, send1, recv1, sendr, recvr,
):
    C, X, Y, Z = dims
    nx, ny, nz = counts
    N = nx * ny * nz
    E = X // 8
    R = 8 * Y
    XY = X * Y
    gx, gy, gz = lax.axis_index("gx"), lax.axis_index("gy"), lax.axis_index("gz")
    me = (gx * ny + gy) * nz + gz
    sh = shift[0]
    lane = lax.broadcasted_iota(jnp.int32, (8, Z), 1)

    def coords(number):
        rest = lax.div(number, nz)
        return (lax.div(rest, ny), lax.rem(rest, ny), lax.rem(number, nz))

    for ref in (zrecv0, xrecv0, yrecv0, erecv0, zrecv, xrecv, yrecv, erecv, esend0, esend):
        ref[...] = jnp.zeros(ref.shape, F32)

    barrier = pltpu.get_barrier_semaphore()

    def greet(i, carry):
        pl.semaphore_signal(
            barrier, inc=1, device_id=coords(lax.rem(me + i, N)), device_id_type=MESH
        )
        return carry

    lax.fori_loop(1, N, greet, 0)

    low_z = gz > 0
    high_z = gz < nz - 1
    low_of = {"x": gx > 0, "y": gy > 0}
    high_of = {"x": gx < nx - 1, "y": gy < ny - 1}
    inner0 = (lane % 8 == 0) & (lane > 0)
    inner7 = (lane % 8 == 7) & (lane < Z - 1)
    rim = (lane == 0) | (lane == Z - 1)

    def assemble(ncols, bufs, sems, par, meanwhile):
        zs, zr, xsn, xr, ysn, yr, es, er = bufs
        ssem, rsem = sems
        for c in range(ncols):
            for e in range(1, E):
                a = (c * X + 8 * e - 1) * Y
                t = lv[a : a + Y] + lv[a + Y : a + 2 * Y]
                lv[a : a + Y] = t
                lv[a + Y : a + 2 * Y] = t
        for k in range(1, Y // 8):
            first = pl.ds(8 * k - 1, ncols * X, stride=Y)
            second = pl.ds(8 * k, ncols * X, stride=Y)
            t = lv[first, :] + lv[second, :]
            lv[first, :] = t
            lv[second, :] = t

        def fold(c, carry):
            packed = jnp.zeros((8, Z), F32)
            for k in range(XY // 8):
                at = pl.ds(pl.multiple_of(c * XY + 8 * k, 8), 8)
                v = lv[at, :]
                v = v + jnp.where(
                    inner0, pltpu.roll(v, 1, 1), jnp.where(inner7, pltpu.roll(v, Z - 1, 1), 0.0)
                )
                lv[at, :] = v
                q = 2 * k
                moved = pltpu.roll(v, q, 1) if q else v
                packed = jnp.where((lane == q) | (lane == (q - 1) % Z), moved, packed)
            zs[pl.ds(pl.multiple_of(8 * c, 8), 8), :] = packed
            return carry

        lax.fori_loop(0, ncols, fold, 0)

        def zcopy(h):
            return pltpu.make_async_remote_copy(
                src_ref=zs,
                dst_ref=zr.at[par, 1 - h],
                send_sem=ssem.at[par, h],
                recv_sem=rsem.at[par, 1 - h],
                device_id=(gx, gy, gz + (2 * h - 1)),
                device_id_type=MESH,
            )

        zgoes = (low_z, high_z)
        for h in range(2):
            @pl.when(zgoes[h])
            def _():
                zcopy(h).start()
        meanwhile()
        for h in range(2):
            @pl.when(zgoes[1 - h])
            def _():
                zcopy(h).wait_recv()

        tiles = Y // 8
        shown = [
            k for k in range(XY // 8)
            if k // tiles in (0, X - 1) or k % tiles in (0, tiles - 1)
        ]
        hidden = [k for k in range(XY // 8) if k not in shown]

        def unfold(picked, c, carry):
            at = pl.ds(pl.multiple_of(8 * c, 8), 8)
            from_low = zr[par, 0, at, :]
            from_high = zr[par, 1, at, :]
            both = jnp.where(
                lane % 2 == 0, pltpu.roll(from_low, 1, 1), pltpu.roll(from_high, Z - 1, 1)
            )
            for k in picked:
                at = pl.ds(pl.multiple_of(c * XY + 8 * k, 8), 8)
                q = (Z - 2 * k) % Z
                moved = pltpu.roll(both, q, 1) if q else both
                lv[at, :] = lv[at, :] + jnp.where(rim, moved, 0.0)
            return carry

        lax.fori_loop(0, ncols, functools.partial(unfold, shown), 0)

        edge = (0, X - 1), (0, Y - 1)
        for h in range(2):
            for c in range(ncols):
                a = (c * X + edge[0][h]) * Y
                xsn[h, c * Y : (c + 1) * Y, :] = lv[a : a + Y]
            ysn[h] = lv[pl.ds(edge[1][h], ncols * X, stride=Y), :]
        for hx in range(2):
            for hy in range(2):
                for c in range(ncols):
                    a = (c * X + edge[0][hx]) * Y + edge[1][hy]
                    es[2 * hx + hy, c : c + 1, :] = lv[a : a + 1, :]

        plans = []
        for h in range(2):
            d = 2 * h - 1
            plans.append((
                (high_of if h else low_of)["x"], (low_of if h else high_of)["x"],
                xsn.at[h], xr.at[par, 1 - h], 2 + h, 2 + (1 - h), (gx + d, gy, gz),
            ))
            plans.append((
                (high_of if h else low_of)["y"], (low_of if h else high_of)["y"],
                ysn.at[h], yr.at[par, 1 - h], 4 + h, 4 + (1 - h), (gx, gy + d, gz),
            ))
        for hx in range(2):
            for hy in range(2):
                goes = (high_of if hx else low_of)["x"] & (high_of if hy else low_of)["y"]
                comes = (low_of if hx else high_of)["x"] & (low_of if hy else high_of)["y"]
                slot = 2 * (1 - hx) + (1 - hy)
                plans.append((
                    goes, comes, es.at[2 * hx + hy], er.at[par, slot],
                    6 + 2 * hx + hy, 6 + slot, (gx + 2 * hx - 1, gy + 2 * hy - 1, gz),
                ))

        def copy_of(plan):
            return pltpu.make_async_remote_copy(
                src_ref=plan[2],
                dst_ref=plan[3],
                send_sem=ssem.at[par, plan[4]],
                recv_sem=rsem.at[par, plan[5]],
                device_id=plan[6],
                device_id_type=MESH,
            )

        for plan in plans:
            @pl.when(plan[0])
            def _():
                copy_of(plan).start()
        if hidden:
            lax.fori_loop(0, ncols, functools.partial(unfold, hidden), 0)
        for plan in plans:
            @pl.when(plan[1])
            def _():
                copy_of(plan).wait_recv()
        for h in range(2):
            for c in range(ncols):
                a = (c * X + edge[0][h]) * Y
                lv[a : a + Y] = lv[a : a + Y] + xr[par, h, c * Y : (c + 1) * Y, :]
            at = pl.ds(edge[1][h], ncols * X, stride=Y)
            lv[at, :] = lv[at, :] + yr[par, h]
        for hx in range(2):
            for hy in range(2):
                for c in range(ncols):
                    a = (c * X + edge[0][hx]) * Y + edge[1][hy]
                    lv[a : a + 1, :] = lv[a : a + 1, :] + er[par, 2 * hx + hy, c : c + 1, :]
        for h in range(2):
            @pl.when(zgoes[h])
            def _():
                zcopy(h).wait_send()
        for plan in plans:
            @pl.when(plan[0])
            def _():
                copy_of(plan).wait_send()

    squares = TABLE * TABLE
    row_of = lax.broadcasted_iota(jnp.int32, (Y, Z), 0)
    lane_of = lax.broadcasted_iota(jnp.int32, (Y, Z), 1)
    at_zero, at_seven = row_of % 8 == 0, row_of % 8 == 7
    ends_y = jnp.where(at_zero, -14.0, jnp.where(at_seven, 14.0, 0.0))
    ends_z = jnp.where(lane_of % 8 == 0, -14.0, jnp.where(lane_of % 8 == 7, 14.0, 0.0))
    wide = jnp.where(at_zero | at_seven, 0.5, 1.0)
    wide = jnp.where((row_of == 0) & (gy == 0), 1.0, wide)
    wide = jnp.where((row_of == Y - 1) & (gy == ny - 1), 1.0, wide)
    deep = jnp.where((lane_of % 8 == 0) | (lane_of % 8 == 7), 0.5, 1.0)
    deep = jnp.where((lane_of == 0) & (gz == 0), 1.0, deep)
    deep = jnp.where((lane_of == Z - 1) & (gz == nz - 1), 1.0, deep)
    plane = wide * deep
    for x in range(X):
        if x == 0:
            factor = jnp.where(gx > 0, 0.5, 1.0)
        elif x == X - 1:
            factor = jnp.where(gx < nx - 1, 0.5, 1.0)
        else:
            factor = 0.5 if x % 8 in (0, 7) else 1.0
        wgt[x * Y : (x + 1) * Y] = plane * factor

    lv[0 : C * XY] = loads[...]
    lv[(C + 1) * XY : (C + 2) * XY] = mass[...]
    for e in range(E):
        base = e * R
        rr[...] = left_apply(ly, 2, metric[1, base : base + R, :]) + right_apply(
            lz, 2, metric[2, base : base + R, :]
        )
        for i in range(8):
            a = base + i * Y
            total = rr[i * Y : (i + 1) * Y] + sh * mass[a : a + Y]
            for m in range(8):
                w = float(np.float32(squares[m, i]))
                if w != 0.0:
                    total = total + w * metric[0, base + m * Y : base + (m + 1) * Y, :]
            cross = ends_y * ends_z * metric[5, a : a + Y, :]
            if i in (0, 7):
                end = -14.0 if i == 0 else 14.0
                cross = cross + end * (
                    ends_y * metric[3, a : a + Y, :] + ends_z * metric[4, a : a + Y, :]
                )
            lv[C * XY + a : C * XY + a + Y] = total + 2.0 * cross
    def clear():
        zero = jnp.zeros((C * XY, Z), F32)
        p[...] = zero
        s[...] = zero
        xs[...] = zero

    rows[...] = jnp.zeros(rows.shape, F32)
    state[...] = jnp.zeros(state.shape, F32)

    pl.semaphore_wait(barrier, N - 1)
    assemble(
        C + 2,
        (zsend0, zrecv0, xsend0, xrecv0, ysend0, yrecv0, esend0, erecv0),
        (send0, recv0), 0, clear,
    )
    rf[...] = lv[0 : C * XY]
    r[...] = lv[0 : C * XY]
    pre[...] = 1.0 / lv[C * XY : (C + 1) * XY]
    mtot[...] = lv[(C + 1) * XY : (C + 2) * XY]
    for c in range(C):
        z[c * XY : (c + 1) * XY] = pre[...] * lv[c * XY : (c + 1) * XY]

    def slab(i, carry):
        c = lax.div(i, E)
        e = i - c * E
        base = pl.multiple_of(i * R, R)
        ebase = pl.multiple_of(e * R, R)
        v = z[pl.ds(base, R), :]
        s2[...] = left_apply(ly, 0, v)
        s3[...] = right_apply(lz, 0, v)
        for t in range(Y // 8):
            va = [z[pl.ds(pl.multiple_of(base + a * Y + 8 * t, 8), 8), :] for a in range(8)]
            s1 = mix_lines(TABLE, va)
            f1 = []
            for m in range(8):
                o = m * Y + 8 * t
                at = pl.ds(pl.multiple_of(ebase + o, 8), 8)
                a, b, g = s1[m], s2[o : o + 8, :], s3[o : o + 8, :]
                m12, m13, m23 = metric[3, at, :], metric[4, at, :], metric[5, at, :]
                f1.append(metric[0, at, :] * a + m12 * b + m13 * g)
                f2[o : o + 8, :] = m12 * a + metric[1, at, :] * b + m23 * g
                f3[o : o + 8, :] = m13 * a + m23 * b + metric[2, at, :] * g
            r1 = mix_lines(TABLE.T, f1)
            for a in range(8):
                o = a * Y + 8 * t
                at = pl.ds(pl.multiple_of(ebase + o, 8), 8)
                rr[o : o + 8, :] = r1[a] + (sh * mass[at, :]) * va[a]
        out = rr[...] + left_apply(ly, 1, f2[...]) + right_apply(lz, 1, f3[...])
        lv[pl.ds(base, R), :] = out
        v = z[pl.ds(base, R), :]
        keep = jnp.where(e == 0, 0.0, 1.0)
        for j in range(C):
            term = fold8(v * inputs[pl.ds(pl.multiple_of(j * XY + ebase, R), R), :])
            acc[C * c + j] = keep * acc[C * c + j] + term
        term = fold8(wgt[pl.ds(ebase, R), :] * (r[pl.ds(base, R), :] * v))
        acc[C * C + c] = keep * acc[C * C + c] + term
        term = fold8(out * v)
        acc[C * C + C + c] = keep * acc[C * C + C + c] + term
        return carry

    def reduce_copy(i, par):
        peer = lax.rem(me + i, N)
        return pltpu.make_async_remote_copy(
            src_ref=asend,
            dst_ref=arecv.at[par, me],
            send_sem=sendr.at[i],
            recv_sem=recvr.at[par, me],
            device_id=coords(peer),
            device_id_type=MESH,
        )

    def arrive_copy(i, par):
        peer = lax.rem(me + i, N)
        return pltpu.make_async_remote_copy(
            src_ref=asend,
            dst_ref=arecv.at[par, peer],
            send_sem=sendr.at[i],
            recv_sem=recvr.at[par, peer],
            device_id=coords(peer),
            device_id_type=MESH,
        )

    def step(number, carry):
        par = lax.rem(number, 2)
        acc[...] = jnp.zeros(acc.shape, F32)
        lax.fori_loop(0, C * E, slab, 0, unroll=2)
        def start_reduction():
            for c in range(C):
                for j in range(C):
                    q = C * c + j
                    rows[q : q + 1, :] = jnp.sum(acc[q], axis=0, keepdims=True)
                energy = jnp.sum(acc[C * C + c], axis=0, keepdims=True)
                curve = jnp.sum(acc[C * C + C + c], axis=0, keepdims=True)
                for j in range(C):
                    q = C * c + j
                    rows[C * C + q : C * C + q + 1, :] = energy
                    rows[2 * C * C + q : 2 * C * C + q + 1, :] = curve
            part = jnp.sum(rows[...].T, axis=0, keepdims=True)
            asend[...] = part
            arecv[par, me] = part

            def push(i, carry):
                reduce_copy(i, par).start()
                return carry

            lax.fori_loop(1, N, push, 0)

        assemble(
            C,
            (zsend, zrecv, xsend, xrecv, ysend, yrecv, esend, erecv),
            (send1, recv1), par, start_reduction,
        )

        for i in range(1, N):
            arrive_copy(i, par).wait_recv()
        total = jnp.sum(arecv[par], axis=0)
        gamma = pltpu.roll(total, 128 - C * C, 1)
        delta = pltpu.roll(total, 128 - 2 * C * C, 1)
        used = lax.broadcasted_iota(jnp.int32, (1, 128), 1) < C * C
        gamma = jnp.where(used, gamma, 1.0)
        delta = jnp.where(used, delta, 1.0)
        fresh = number == 0
        old_gamma = jnp.where(fresh, 1.0, state[0:1, :])
        old_alpha = jnp.where(fresh, 1.0, state[1:2, :])
        beta = jnp.where(fresh, 0.0, gamma / old_gamma)
        alpha = gamma / (delta - beta * gamma / old_alpha)
        along = total + beta * state[2:3, :]
        state[0:1, :] = gamma
        state[1:2, :] = alpha
        state[2:3, :] = along
        state[3:4, :] = state[3:4, :] + alpha * along
        for c in range(C):
            b = jnp.broadcast_to(beta[:, C * c : C * c + 1], (Y, Z))
            a = jnp.broadcast_to(alpha[:, C * c : C * c + 1], (Y, Z))
            def update(x, carry):
                at = pl.ds(pl.multiple_of(c * XY + x * Y, Y), Y)
                pn = z[at, :] + b * p[at, :]
                sn = lv[at, :] + b * s[at, :]
                p[at, :] = pn
                s[at, :] = sn
                xs[at, :] = xs[at, :] + a * pn
                rn = r[at, :] - a * sn
                r[at, :] = rn
                z[at, :] = pre[pl.ds(pl.multiple_of(x * Y, Y), Y), :] * rn
                return carry
            lax.fori_loop(0, X, update, 0, unroll=4)

        for i in range(1, N):
            reduce_copy(i, par).wait_send()
        return carry

    lax.fori_loop(0, STEPS, step, 0)

    flat = state[3:4, :]
    k = [
        [jnp.broadcast_to(flat[:, C * c + j : C * c + j + 1], (8, Z)) for j in range(C)]
        for c in range(C)
    ]
    y = [[None] * C for _ in range(C)]
    for a in range(C):
        for b in range(C):
            if b < a:
                y[a][b] = y[b][a]
                continue
            t = k[a][0] * k[b][0]
            for j in range(1, C):
                t = t + k[a][j] * k[b][j]
            y[a][b] = t + 1.0 if a == b else t
    one = jnp.ones((8, Z), F32)
    nil = jnp.zeros((8, Z), F32)
    right = [[one if a == b else nil for b in range(C)] + k[a] for a in range(C)]
    for a in range(C):
        inv = 1.0 / y[a][a]
        y[a] = [t * inv for t in y[a]]
        right[a] = [t * inv for t in right[a]]
        for b in range(C):
            if b != a:
                w = y[b][a]
                y[b] = [u - w * t for u, t in zip(y[b], y[a])]
                right[b] = [u - w * t for u, t in zip(right[b], right[a])]
    twice = 2.0 * sh
    coef = [[twice * right[c][j] for j in range(2 * C)] for c in range(C)]

    def finish(i, carry):
        at = pl.ds(pl.multiple_of(8 * i, 8), 8)
        m = mtot[at, :]
        heat = [m * xs[pl.ds(pl.multiple_of(c * XY + 8 * i, 8), 8), :] for c in range(C)]
        for j in range(C):
            at = pl.ds(pl.multiple_of(j * XY + 8 * i, 8), 8)
            t = heat[0] * coef[0][j]
            u = heat[0] * coef[0][C + j]
            for c in range(1, C):
                t = t + heat[c] * coef[c][j]
                u = u + heat[c] * coef[c][C + j]
            rf[at, :] = rf[at, :] - t
            fb[at, :] = u
        return carry

    lax.fori_loop(0, XY // 8, finish, 0, unroll=2)


def local(counts, metric, mass, shift, loads, inputs):
    C, X, Y, Z = loads.shape
    N = counts[0] * counts[1] * counts[2]
    XY = X * Y
    ly = jnp.asarray(left_matrices(Y))
    lz = jnp.asarray(right_matrices(Z))
    vm = lambda *shape: pltpu.VMEM(shape, F32)

    def comm(cols, pars):
        return [
            vm(8 * cols, Z), vm(pars, 2, 8 * cols, Z),
            vm(2, cols * Y, Z), vm(pars, 2, cols * Y, Z),
            vm(2, cols * X, Z), vm(pars, 2, cols * X, Z),
            vm(4, 8, Z), vm(pars, 4, 8, Z),
        ]

    dma = pltpu.SemaphoreType.DMA
    spec = pl.BlockSpec(memory_space=pltpu.VMEM)
    rf, fb = pl.pallas_call(
        functools.partial(kernel, (C, X, Y, Z), counts),
        out_shape=[jax.ShapeDtypeStruct((C * XY, Z), F32)] * 2,
        in_specs=[spec, spec, pl.BlockSpec(memory_space=pltpu.SMEM), spec, spec, spec, spec],
        out_specs=[spec, spec],
        scratch_shapes=[
            vm((C + 2) * XY, Z), vm(C * XY, Z), vm(C * XY, Z), vm(C * XY, Z), vm(C * XY, Z),
            vm(C * XY, Z), vm(XY, Z), vm(XY, Z), vm(XY, Z),
            vm(8 * Y, Z), vm(8 * Y, Z), vm(8 * Y, Z), vm(8 * Y, Z), vm(8 * Y, Z),
            vm(C * C + 2 * C, 8, Z), vm(128, Z), vm(8, 128),
        ]
        + comm(C + 2, 1)
        + comm(C, 2)
        + [vm(1, 128), vm(2, N, 1, 128)]
        + [dma((1, 10)), dma((1, 10)), dma((2, 10)), dma((2, 10)), dma((N,)), dma((2, N))],
        compiler_params=pltpu.CompilerParams(
            collective_id=0, has_side_effects=True, vmem_limit_bytes=56 << 20
        ),
    )(
        metric.reshape(6, XY, Z), mass.reshape(XY, Z), shift,
        loads.reshape(C * XY, Z), inputs.reshape(C * XY, Z), ly, lz,
    )
    return (rf.reshape(loads.shape), fb.reshape(loads.shape))


def solution(mesh):
    counts = tuple(mesh.shape[a] for a in ("gx", "gy", "gz"))
    return jax.shard_map(
        functools.partial(local, counts),
        mesh=mesh,
        in_specs=(
            P(None, "gx", "gy", "gz"),
            P("gx", "gy", "gz"),
            P(),
            P(None, "gx", "gy", "gz"),
            P(None, "gx", "gy", "gz"),
        ),
        out_specs=(P(None, "gx", "gy", "gz"), P(None, "gx", "gy", "gz")),
        check_vma=False,
    )
```

```python
import functools

import jax
import jax.numpy as jnp
import numpy as np
from jax import lax
from jax.experimental import pallas as pl
from jax.experimental.pallas import tpu as pltpu
from jax.sharding import PartitionSpec as P

STEPS = 5
MESH = pl.DeviceIdType.MESH
F32 = jnp.float32
BF16 = jnp.bfloat16

gll_points = (
    -1.0,
    -0.8717401485096066,
    -0.5917001814331423,
    -0.2092992179024789,
    0.2092992179024789,
    0.5917001814331423,
    0.8717401485096066,
    1.0,
)


def gll_table():
    points = np.array(gll_points)
    values = (429.0 * points**7 - 693.0 * points**5 + 315.0 * points**3 - 35.0 * points) / 16.0
    table = np.zeros((8, 8))
    for row in range(8):
        for column in range(8):
            if row != column:
                table[row, column] = values[row] / (values[column] * (points[row] - points[column]))
    table[0, 0] = -14.0
    table[7, 7] = 14.0
    return table


TABLE = gll_table()


def halves(matrix):
    full = np.asarray(matrix, np.float32)
    high = full.astype(jnp.bfloat16)
    low = (full - high.astype(np.float32)).astype(jnp.bfloat16)
    return high, low


def left_matrices(height):
    eye = np.eye(height)
    squares = TABLE * TABLE
    return np.stack([np.stack(halves(np.kron(eye, m))) for m in (TABLE, TABLE.T, squares.T)])


def right_matrices(depth):
    eye = np.eye(depth // 8)
    squares = TABLE * TABLE
    out = []
    for m in (TABLE.T, TABLE, squares):
        high, low = halves(np.kron(eye, m))
        out.append(np.block([[high, low], [high, np.zeros_like(low)]]))
    return np.stack(out)


def mix_lines(matrix, lines):
    even = [lines[j] + lines[7 - j] for j in range(4)]
    odd = [lines[j] - lines[7 - j] for j in range(4)]
    out = [None] * 8
    for i in range(4):
        p = q = None
        for j in range(4):
            a = float(np.float32(0.5 * (matrix[i, j] + matrix[i, 7 - j])))
            b = float(np.float32(0.5 * (matrix[i, j] - matrix[i, 7 - j])))
            p = a * even[j] if p is None else p + a * even[j]
            q = b * odd[j] if q is None else q + b * odd[j]
        out[i] = q + p
        out[7 - i] = q - p
    return out


def split(v):
    high = v.astype(BF16)
    low = (v - high.astype(F32)).astype(BF16)
    return high, low


def dot(a, b):
    return jnp.dot(a, b, preferred_element_type=F32)


def left_apply(ly, kind, v):
    high, low = split(v)
    return (dot(ly[kind, 0], low) + dot(ly[kind, 1], high)) + dot(ly[kind, 0], high)


def right_apply(lz, kind, v):
    high, low = split(v)
    depth = v.shape[1]
    both = dot(jnp.concatenate([high, low], axis=1), lz[kind])
    return both[:, :depth] + both[:, depth:]


def fold8(v):
    total = v[0:8]
    for k in range(1, v.shape[0] // 8):
        total = total + v[8 * k : 8 * k + 8]
    return total


def kernel(
    dims, counts,
    metric, mass, shift, loads, inputs, ly, lz,
    rf, fb,
    lv, z, p, s, xs, r, wgt, pre, mtot, s2, s3, f2, f3, rr, acc, rows, state,
    zsend0, zrecv0, xsend0, xrecv0, ysend0, yrecv0, esend0, erecv0,
    zsend, zrecv, xsend, xrecv, ysend, yrecv, esend, erecv,
    asend, arecv,
    send0, recv0, send1, recv1, sendr, recvr,
):
    C, X, Y, Z = dims
    nx, ny, nz = counts
    N = nx * ny * nz
    E = X // 8
    R = 8 * Y
    XY = X * Y
    gx, gy, gz = lax.axis_index("gx"), lax.axis_index("gy"), lax.axis_index("gz")
    me = (gx * ny + gy) * nz + gz
    sh = shift[0]
    lane = lax.broadcasted_iota(jnp.int32, (8, Z), 1)

    def coords(number):
        rest = lax.div(number, nz)
        return (lax.div(rest, ny), lax.rem(rest, ny), lax.rem(number, nz))

    for ref in (zrecv0, xrecv0, yrecv0, erecv0, zrecv, xrecv, yrecv, erecv, esend0, esend):
        ref[...] = jnp.zeros(ref.shape, F32)

    barrier = pltpu.get_barrier_semaphore()

    def greet(i, carry):
        pl.semaphore_signal(
            barrier, inc=1, device_id=coords(lax.rem(me + i, N)), device_id_type=MESH
        )
        return carry

    lax.fori_loop(1, N, greet, 0)

    low_z = gz > 0
    high_z = gz < nz - 1
    low_of = {"x": gx > 0, "y": gy > 0}
    high_of = {"x": gx < nx - 1, "y": gy < ny - 1}
    inner0 = (lane % 8 == 0) & (lane > 0)
    inner7 = (lane % 8 == 7) & (lane < Z - 1)
    rim = (lane == 0) | (lane == Z - 1)

    def assemble(ncols, bufs, sems, par, meanwhile):
        zs, zr, xsn, xr, ysn, yr, es, er = bufs
        ssem, rsem = sems
        for c in range(ncols):
            for e in range(1, E):
                a = (c * X + 8 * e - 1) * Y
                t = lv[a : a + Y] + lv[a + Y : a + 2 * Y]
                lv[a : a + Y] = t
                lv[a + Y : a + 2 * Y] = t
        for k in range(1, Y // 8):
            first = pl.ds(8 * k - 1, ncols * X, stride=Y)
            second = pl.ds(8 * k, ncols * X, stride=Y)
            t = lv[first, :] + lv[second, :]
            lv[first, :] = t
            lv[second, :] = t

        def fold(c, carry):
            packed = jnp.zeros((8, Z), F32)
            for k in range(XY // 8):
                at = pl.ds(pl.multiple_of(c * XY + 8 * k, 8), 8)
                v = lv[at, :]
                v = v + jnp.where(
                    inner0, pltpu.roll(v, 1, 1), jnp.where(inner7, pltpu.roll(v, Z - 1, 1), 0.0)
                )
                lv[at, :] = v
                q = 2 * k
                moved = pltpu.roll(v, q, 1) if q else v
                packed = jnp.where((lane == q) | (lane == (q - 1) % Z), moved, packed)
            zs[pl.ds(pl.multiple_of(8 * c, 8), 8), :] = packed
            return carry

        lax.fori_loop(0, ncols, fold, 0, unroll=2)

        def zcopy(h):
            return pltpu.make_async_remote_copy(
                src_ref=zs,
                dst_ref=zr.at[par, 1 - h],
                send_sem=ssem.at[par, h],
                recv_sem=rsem.at[par, 1 - h],
                device_id=(gx, gy, gz + (2 * h - 1)),
                device_id_type=MESH,
            )

        zgoes = (low_z, high_z)
        for h in range(2):
            @pl.when(zgoes[h])
            def _():
                zcopy(h).start()
        meanwhile()
        for h in range(2):
            @pl.when(zgoes[1 - h])
            def _():
                zcopy(h).wait_recv()

        tiles = Y // 8
        shown = [
            k for k in range(XY // 8)
            if k // tiles in (0, X - 1) or k % tiles in (0, tiles - 1)
        ]
        hidden = [k for k in range(XY // 8) if k not in shown]

        def unfold(picked, c, carry):
            at = pl.ds(pl.multiple_of(8 * c, 8), 8)
            from_low = zr[par, 0, at, :]
            from_high = zr[par, 1, at, :]
            both = jnp.where(
                lane % 2 == 0, pltpu.roll(from_low, 1, 1), pltpu.roll(from_high, Z - 1, 1)
            )
            for k in picked:
                at = pl.ds(pl.multiple_of(c * XY + 8 * k, 8), 8)
                q = (Z - 2 * k) % Z
                moved = pltpu.roll(both, q, 1) if q else both
                lv[at, :] = lv[at, :] + jnp.where(rim, moved, 0.0)
            return carry

        lax.fori_loop(0, ncols, functools.partial(unfold, shown), 0, unroll=2)

        edge = (0, X - 1), (0, Y - 1)
        for h in range(2):
            for c in range(ncols):
                a = (c * X + edge[0][h]) * Y
                xsn[h, c * Y : (c + 1) * Y, :] = lv[a : a + Y]
            ysn[h] = lv[pl.ds(edge[1][h], ncols * X, stride=Y), :]
        for hx in range(2):
            for hy in range(2):
                for c in range(ncols):
                    a = (c * X + edge[0][hx]) * Y + edge[1][hy]
                    es[2 * hx + hy, c : c + 1, :] = lv[a : a + 1, :]

        plans = []
        for h in range(2):
            d = 2 * h - 1
            plans.append((
                (high_of if h else low_of)["x"], (low_of if h else high_of)["x"],
                xsn.at[h], xr.at[par, 1 - h], 2 + h, 2 + (1 - h), (gx + d, gy, gz),
            ))
            plans.append((
                (high_of if h else low_of)["y"], (low_of if h else high_of)["y"],
                ysn.at[h], yr.at[par, 1 - h], 4 + h, 4 + (1 - h), (gx, gy + d, gz),
            ))
        for hx in range(2):
            for hy in range(2):
                goes = (high_of if hx else low_of)["x"] & (high_of if hy else low_of)["y"]
                comes = (low_of if hx else high_of)["x"] & (low_of if hy else high_of)["y"]
                slot = 2 * (1 - hx) + (1 - hy)
                plans.append((
                    goes, comes, es.at[2 * hx + hy], er.at[par, slot],
                    6 + 2 * hx + hy, 6 + slot, (gx + 2 * hx - 1, gy + 2 * hy - 1, gz),
                ))

        def copy_of(plan):
            return pltpu.make_async_remote_copy(
                src_ref=plan[2],
                dst_ref=plan[3],
                send_sem=ssem.at[par, plan[4]],
                recv_sem=rsem.at[par, plan[5]],
                device_id=plan[6],
                device_id_type=MESH,
            )

        for plan in plans:
            @pl.when(plan[0])
            def _():
                copy_of(plan).start()
        if hidden:
            lax.fori_loop(0, ncols, functools.partial(unfold, hidden), 0, unroll=2)
        for plan in plans:
            @pl.when(plan[1])
            def _():
                copy_of(plan).wait_recv()
        for h in range(2):
            for c in range(ncols):
                a = (c * X + edge[0][h]) * Y
                lv[a : a + Y] = lv[a : a + Y] + xr[par, h, c * Y : (c + 1) * Y, :]
            at = pl.ds(edge[1][h], ncols * X, stride=Y)
            lv[at, :] = lv[at, :] + yr[par, h]
        for hx in range(2):
            for hy in range(2):
                for c in range(ncols):
                    a = (c * X + edge[0][hx]) * Y + edge[1][hy]
                    lv[a : a + 1, :] = lv[a : a + 1, :] + er[par, 2 * hx + hy, c : c + 1, :]
        for h in range(2):
            @pl.when(zgoes[h])
            def _():
                zcopy(h).wait_send()
        for plan in plans:
            @pl.when(plan[0])
            def _():
                copy_of(plan).wait_send()

    squares = TABLE * TABLE
    row_of = lax.broadcasted_iota(jnp.int32, (Y, Z), 0)
    lane_of = lax.broadcasted_iota(jnp.int32, (Y, Z), 1)
    at_zero, at_seven = row_of % 8 == 0, row_of % 8 == 7
    ends_y = jnp.where(at_zero, -14.0, jnp.where(at_seven, 14.0, 0.0))
    ends_z = jnp.where(lane_of % 8 == 0, -14.0, jnp.where(lane_of % 8 == 7, 14.0, 0.0))
    wide = jnp.where(at_zero | at_seven, 0.5, 1.0)
    wide = jnp.where((row_of == 0) & (gy == 0), 1.0, wide)
    wide = jnp.where((row_of == Y - 1) & (gy == ny - 1), 1.0, wide)
    deep = jnp.where((lane_of % 8 == 0) | (lane_of % 8 == 7), 0.5, 1.0)
    deep = jnp.where((lane_of == 0) & (gz == 0), 1.0, deep)
    deep = jnp.where((lane_of == Z - 1) & (gz == nz - 1), 1.0, deep)
    plane = wide * deep
    for x in range(X):
        if x == 0:
            factor = jnp.where(gx > 0, 0.5, 1.0)
        elif x == X - 1:
            factor = jnp.where(gx < nx - 1, 0.5, 1.0)
        else:
            factor = 0.5 if x % 8 in (0, 7) else 1.0
        wgt[x * Y : (x + 1) * Y] = plane * factor

    lv[0 : C * XY] = loads[...]
    lv[(C + 1) * XY : (C + 2) * XY] = mass[...]
    for e in range(E):
        base = e * R
        rr[...] = left_apply(ly, 2, metric[1, base : base + R, :]) + right_apply(
            lz, 2, metric[2, base : base + R, :]
        )
        for i in range(8):
            a = base + i * Y
            total = rr[i * Y : (i + 1) * Y] + sh * mass[a : a + Y]
            for m in range(8):
                w = float(np.float32(squares[m, i]))
                if w != 0.0:
                    total = total + w * metric[0, base + m * Y : base + (m + 1) * Y, :]
            cross = ends_y * ends_z * metric[5, a : a + Y, :]
            if i in (0, 7):
                end = -14.0 if i == 0 else 14.0
                cross = cross + end * (
                    ends_y * metric[3, a : a + Y, :] + ends_z * metric[4, a : a + Y, :]
                )
            lv[C * XY + a : C * XY + a + Y] = total + 2.0 * cross
    def clear():
        zero = jnp.zeros((C * XY, Z), F32)
        p[...] = zero
        s[...] = zero
        xs[...] = zero

    rows[...] = jnp.zeros(rows.shape, F32)
    state[...] = jnp.zeros(state.shape, F32)

    pl.semaphore_wait(barrier, N - 1)
    assemble(
        C + 2,
        (zsend0, zrecv0, xsend0, xrecv0, ysend0, yrecv0, esend0, erecv0),
        (send0, recv0), 0, clear,
    )
    rf[...] = lv[0 : C * XY]
    r[...] = lv[0 : C * XY]
    pre[...] = 1.0 / lv[C * XY : (C + 1) * XY]
    mtot[...] = lv[(C + 1) * XY : (C + 2) * XY]
    for c in range(C):
        z[c * XY : (c + 1) * XY] = pre[...] * lv[c * XY : (c + 1) * XY]

    def slab(i, carry):
        c = lax.div(i, E)
        e = i - c * E
        base = pl.multiple_of(i * R, R)
        ebase = pl.multiple_of(e * R, R)
        v = z[pl.ds(base, R), :]
        s2[...] = left_apply(ly, 0, v)
        s3[...] = right_apply(lz, 0, v)
        for t in range(Y // 8):
            va = [z[pl.ds(pl.multiple_of(base + a * Y + 8 * t, 8), 8), :] for a in range(8)]
            s1 = mix_lines(TABLE, va)
            f1 = []
            for m in range(8):
                o = m * Y + 8 * t
                at = pl.ds(pl.multiple_of(ebase + o, 8), 8)
                a, b, g = s1[m], s2[o : o + 8, :], s3[o : o + 8, :]
                m12, m13, m23 = metric[3, at, :], metric[4, at, :], metric[5, at, :]
                f1.append(metric[0, at, :] * a + m12 * b + m13 * g)
                f2[o : o + 8, :] = m12 * a + metric[1, at, :] * b + m23 * g
                f3[o : o + 8, :] = m13 * a + m23 * b + metric[2, at, :] * g
            r1 = mix_lines(TABLE.T, f1)
            for a in range(8):
                o = a * Y + 8 * t
                at = pl.ds(pl.multiple_of(ebase + o, 8), 8)
                rr[o : o + 8, :] = r1[a] + (sh * mass[at, :]) * va[a]
        out = rr[...] + left_apply(ly, 1, f2[...]) + right_apply(lz, 1, f3[...])
        lv[pl.ds(base, R), :] = out
        v = z[pl.ds(base, R), :]
        keep = jnp.where(e == 0, 0.0, 1.0)
        for j in range(C):
            term = fold8(v * inputs[pl.ds(pl.multiple_of(j * XY + ebase, R), R), :])
            acc[C * c + j] = keep * acc[C * c + j] + term
        term = fold8(wgt[pl.ds(ebase, R), :] * (r[pl.ds(base, R), :] * v))
        acc[C * C + c] = keep * acc[C * C + c] + term
        term = fold8(out * v)
        acc[C * C + C + c] = keep * acc[C * C + C + c] + term
        return carry

    def reduce_copy(i, par):
        peer = lax.rem(me + i, N)
        return pltpu.make_async_remote_copy(
            src_ref=asend,
            dst_ref=arecv.at[par, me],
            send_sem=sendr.at[i],
            recv_sem=recvr.at[par, me],
            device_id=coords(peer),
            device_id_type=MESH,
        )

    def arrive_copy(i, par):
        peer = lax.rem(me + i, N)
        return pltpu.make_async_remote_copy(
            src_ref=asend,
            dst_ref=arecv.at[par, peer],
            send_sem=sendr.at[i],
            recv_sem=recvr.at[par, peer],
            device_id=coords(peer),
            device_id_type=MESH,
        )

    def step(number, carry):
        par = lax.rem(number, 2)
        acc[...] = jnp.zeros(acc.shape, F32)
        lax.fori_loop(0, C * E, slab, 0, unroll=4)
        def start_reduction():
            for c in range(C):
                for j in range(C):
                    q = C * c + j
                    rows[q : q + 1, :] = jnp.sum(acc[q], axis=0, keepdims=True)
                energy = jnp.sum(acc[C * C + c], axis=0, keepdims=True)
                curve = jnp.sum(acc[C * C + C + c], axis=0, keepdims=True)
                for j in range(C):
                    q = C * c + j
                    rows[C * C + q : C * C + q + 1, :] = energy
                    rows[2 * C * C + q : 2 * C * C + q + 1, :] = curve
            part = jnp.sum(rows[...].T, axis=0, keepdims=True)
            asend[...] = part
            arecv[par, me] = part

            def push(i, carry):
                reduce_copy(i, par).start()
                return carry

            lax.fori_loop(1, N, push, 0)

        assemble(
            C,
            (zsend, zrecv, xsend, xrecv, ysend, yrecv, esend, erecv),
            (send1, recv1), par, start_reduction,
        )

        for i in range(1, N):
            arrive_copy(i, par).wait_recv()
        total = jnp.sum(arecv[par], axis=0)
        gamma = pltpu.roll(total, 128 - C * C, 1)
        delta = pltpu.roll(total, 128 - 2 * C * C, 1)
        used = lax.broadcasted_iota(jnp.int32, (1, 128), 1) < C * C
        gamma = jnp.where(used, gamma, 1.0)
        delta = jnp.where(used, delta, 1.0)
        fresh = number == 0
        old_gamma = jnp.where(fresh, 1.0, state[0:1, :])
        old_alpha = jnp.where(fresh, 1.0, state[1:2, :])
        beta = jnp.where(fresh, 0.0, gamma / old_gamma)
        alpha = gamma / (delta - beta * gamma / old_alpha)
        along = total + beta * state[2:3, :]
        state[0:1, :] = gamma
        state[1:2, :] = alpha
        state[2:3, :] = along
        state[3:4, :] = state[3:4, :] + alpha * along
        for c in range(C):
            b = jnp.broadcast_to(beta[:, C * c : C * c + 1], (Y, Z))
            a = jnp.broadcast_to(alpha[:, C * c : C * c + 1], (Y, Z))
            def update(x, carry):
                at = pl.ds(pl.multiple_of(c * XY + x * Y, Y), Y)
                pn = z[at, :] + b * p[at, :]
                sn = lv[at, :] + b * s[at, :]
                p[at, :] = pn
                s[at, :] = sn
                xs[at, :] = xs[at, :] + a * pn
                rn = r[at, :] - a * sn
                r[at, :] = rn
                z[at, :] = pre[pl.ds(pl.multiple_of(x * Y, Y), Y), :] * rn
                return carry
            lax.fori_loop(0, X, update, 0, unroll=8)

        for i in range(1, N):
            reduce_copy(i, par).wait_send()
        return carry

    lax.fori_loop(0, STEPS, step, 0)

    flat = state[3:4, :]
    k = [
        [jnp.broadcast_to(flat[:, C * c + j : C * c + j + 1], (8, Z)) for j in range(C)]
        for c in range(C)
    ]
    y = [[None] * C for _ in range(C)]
    for a in range(C):
        for b in range(C):
            if b < a:
                y[a][b] = y[b][a]
                continue
            t = k[a][0] * k[b][0]
            for j in range(1, C):
                t = t + k[a][j] * k[b][j]
            y[a][b] = t + 1.0 if a == b else t
    one = jnp.ones((8, Z), F32)
    nil = jnp.zeros((8, Z), F32)
    right = [[one if a == b else nil for b in range(C)] + k[a] for a in range(C)]
    for a in range(C):
        inv = 1.0 / y[a][a]
        y[a] = [t * inv for t in y[a]]
        right[a] = [t * inv for t in right[a]]
        for b in range(C):
            if b != a:
                w = y[b][a]
                y[b] = [u - w * t for u, t in zip(y[b], y[a])]
                right[b] = [u - w * t for u, t in zip(right[b], right[a])]
    twice = 2.0 * sh
    coef = [[twice * right[c][j] for j in range(2 * C)] for c in range(C)]

    def finish(i, carry):
        at = pl.ds(pl.multiple_of(8 * i, 8), 8)
        m = mtot[at, :]
        heat = [m * xs[pl.ds(pl.multiple_of(c * XY + 8 * i, 8), 8), :] for c in range(C)]
        for j in range(C):
            at = pl.ds(pl.multiple_of(j * XY + 8 * i, 8), 8)
            t = heat[0] * coef[0][j]
            u = heat[0] * coef[0][C + j]
            for c in range(1, C):
                t = t + heat[c] * coef[c][j]
                u = u + heat[c] * coef[c][C + j]
            rf[at, :] = rf[at, :] - t
            fb[at, :] = u
        return carry

    lax.fori_loop(0, XY // 8, finish, 0, unroll=2)


def local(counts, metric, mass, shift, loads, inputs):
    C, X, Y, Z = loads.shape
    N = counts[0] * counts[1] * counts[2]
    XY = X * Y
    ly = jnp.asarray(left_matrices(Y))
    lz = jnp.asarray(right_matrices(Z))
    vm = lambda *shape: pltpu.VMEM(shape, F32)

    def comm(cols, pars):
        return [
            vm(8 * cols, Z), vm(pars, 2, 8 * cols, Z),
            vm(2, cols * Y, Z), vm(pars, 2, cols * Y, Z),
            vm(2, cols * X, Z), vm(pars, 2, cols * X, Z),
            vm(4, 8, Z), vm(pars, 4, 8, Z),
        ]

    dma = pltpu.SemaphoreType.DMA
    spec = pl.BlockSpec(memory_space=pltpu.VMEM)
    rf, fb = pl.pallas_call(
        functools.partial(kernel, (C, X, Y, Z), counts),
        out_shape=[jax.ShapeDtypeStruct((C * XY, Z), F32)] * 2,
        in_specs=[spec, spec, pl.BlockSpec(memory_space=pltpu.SMEM), spec, spec, spec, spec],
        out_specs=[spec, spec],
        scratch_shapes=[
            vm((C + 2) * XY, Z), vm(C * XY, Z), vm(C * XY, Z), vm(C * XY, Z), vm(C * XY, Z),
            vm(C * XY, Z), vm(XY, Z), vm(XY, Z), vm(XY, Z),
            vm(8 * Y, Z), vm(8 * Y, Z), vm(8 * Y, Z), vm(8 * Y, Z), vm(8 * Y, Z),
            vm(C * C + 2 * C, 8, Z), vm(128, Z), vm(8, 128),
        ]
        + comm(C + 2, 1)
        + comm(C, 2)
        + [vm(1, 128), vm(2, N, 1, 128)]
        + [dma((1, 10)), dma((1, 10)), dma((2, 10)), dma((2, 10)), dma((N,)), dma((2, N))],
        compiler_params=pltpu.CompilerParams(
            collective_id=0, has_side_effects=True, vmem_limit_bytes=56 << 20
        ),
    )(
        metric.reshape(6, XY, Z), mass.reshape(XY, Z), shift,
        loads.reshape(C * XY, Z), inputs.reshape(C * XY, Z), ly, lz,
    )
    return (rf.reshape(loads.shape), fb.reshape(loads.shape))


def solution(mesh):
    counts = tuple(mesh.shape[a] for a in ("gx", "gy", "gz"))
    return jax.shard_map(
        functools.partial(local, counts),
        mesh=mesh,
        in_specs=(
            P(None, "gx", "gy", "gz"),
            P("gx", "gy", "gz"),
            P(),
            P(None, "gx", "gy", "gz"),
            P(None, "gx", "gy", "gz"),
        ),
        out_specs=(P(None, "gx", "gy", "gz"), P(None, "gx", "gy", "gz")),
        check_vma=False,
    )
```
